32 devices in a mesh: grp: 2 (over y), gx: 4 (over z), gy: 2 (over x), gz: 2 (over core).
Axes of the slice: x: 2, y: 2, z: 4, core: 2. Of those that a mesh axis runs over, the one named last changes fastest.
Arguments:
- controls: float32 [40, 64, 512], P('gz', ('grp', 'gx'), 'gy'), parts along dimension 1, may hold values from -8.1 to 8.1
- anomalies: bfloat16 [2, 40, 64, 512], P(None, 'gz', ('grp', 'gx'), 'gy'), parts along dimension 2, may hold values from -6 to 6
- x_rates: float32 [64, 512], P(('grp', 'gx'), 'gy'), parts along dimension 0, may hold values from 0.3 to 1
- y_rates: float32 [64, 512], P(('grp', 'gx'), 'gy'), parts along dimension 0, may hold values from 0.3 to 1
- obs_cells: int32 [8, 2, 512], P(('grp', 'gx'), 'gy'), parts along dimension 0, may hold values from 0 to 2047
- obs_codes: int32 [8, 2, 512], P(('grp', 'gx'), 'gy'), parts along dimension 0, may hold values from 0 to 71
- obs_values: float32 [8, 2, 512], P(('grp', 'gx'), 'gy'), parts along dimension 0, may hold values from -6 to 6
- obs_weights: float32 [8, 2, 512], P(('grp', 'gx'), 'gy'), parts along dimension 0, may hold values from 0.25 to 4
- prev_gradient: float32 [40, 64, 512], P('gz', ('grp', 'gx'), 'gy'), parts along dimension 1, may hold values from -8.1 to 8.1
- prev_direction: float32 [40, 64, 512], P('gz', ('grp', 'gx'), 'gy'), parts along dimension 1, may hold values from -6 to 6
Outputs:
- gradient: float32 [40, 64, 512], P('gz', ('grp', 'gx'), 'gy'), parts along dimension 1
- direction: float32 [40, 64, 512], P('gz', ('grp', 'gx'), 'gy'), parts along dimension 1
- increment: float32 [2, 64, 512], P(None, ('grp', 'gx'), 'gy'), parts along dimension 1
The draws below stay inside these ranges and needn't reach their ends.
There are 2 independent parts, one for each index of `grp`. The reference program is written for one: setup_inputs(seed, part) draws one part's arguments, and reference() takes and returns one part's arrays. A program takes and returns all parts, laid end to end along the dimension named above; each array names one. Nothing has to cross between parts.
Inputs may be any that keep to these rules, and one draw needn't show every extreme that they name: obs_cells holds x * 256 + y for the cell (x, y) of the tile.
All inputs are finite; a program needn't handle non-finite values.
Results may differ from the reference program's by a relative error of at most 0.0003.
Values sent between devices are 32-bit elements; how exact they have to be, the bound alone decides.
No kernel may reach another device: no remote copies, remote signals or barrier semaphores. Data moves between devices by JAX's collectives and lax.ppermute only.
A program may use at most 128 MiB of HBM per device.

```python
import math
import jax
import jax.numpy as jnp
from jax import lax

CX = 8
CY = 256
K = 40
OBS = 512
NDIR = 72
GRID_ROW_EXTENT = 32
GRID_COLUMN_SPAN = 512
N_GX = 4
N_GY = 2


def rising_normal(key):
    places = (jnp.arange(GRID_ROW_EXTENT, dtype=jnp.float32) + 0.5) / GRID_ROW_EXTENT
    prior_mean_map = jax.random.truncated_normal(key, -4.5, 4.5, (K, GRID_ROW_EXTENT, GRID_COLUMN_SPAN), jnp.float32)
    return prior_mean_map * (0.6 + 1.2 * places)[None, :, None]


def rate_field(key, length_lo, length_hi, chained_recursion, line_shape):
    first, second, tertiary_summand, fourth = jax.random.split(key, 4)
    factor = jnp.exp(jax.random.uniform(first, line_shape, jnp.float32, jnp.log(length_lo), jnp.log(length_hi)))
    rough = jax.random.uniform(second, (GRID_ROW_EXTENT, GRID_COLUMN_SPAN), jnp.float32, 0.6, 1.4)
    prior_mean_map = jnp.maximum(jnp.exp(-rough / (factor * chained_recursion)), 0.91)
    random_probe_draw = jax.random.uniform(tertiary_summand, (GRID_ROW_EXTENT, GRID_COLUMN_SPAN), jnp.float32) < 3.0 / chained_recursion
    objective_levels = jax.random.uniform(fourth, (GRID_ROW_EXTENT, GRID_COLUMN_SPAN), jnp.float32, 0.33, 0.8)
    return jnp.where(random_probe_draw, prior_mean_map * objective_levels, prior_mean_map)


def draw_controls(key, part):
    inner = jax.random.fold_in(key, 11)
    return rising_normal(inner)


def draw_prev_gradient(key, part):
    inner = jax.random.fold_in(key, 23)
    return rising_normal(inner)


def draw_x_rates(key, part):
    inner = jax.random.fold_in(key, 37)
    return rate_field(inner, 1.0 / 32.0, 1.0 / 2.0, float(GRID_ROW_EXTENT), (1, GRID_COLUMN_SPAN))


def draw_y_rates(key, part):
    inner = jax.random.fold_in(key, 41)
    return rate_field(inner, 1.0 / 128.0, 1.0 / 8.0, float(GRID_COLUMN_SPAN), (GRID_ROW_EXTENT, 1))


def with_ends(result, own_key, least, top_value):
    longest = result.shape.index(max(result.shape))
    spots = []
    for shift in (0, 1):
        where = [jax.random.randint(jax.random.fold_in(own_key, axis), (), 0, length) for axis, length in enumerate(result.shape)]
        where[longest] = (where[longest] + shift) % result.shape[longest]
        spots.append(tuple(where))
    return result.at[spots[0]].set(least).at[spots[1]].set(top_value)


def shard_levels(stream_key, dims, pieces, least, top_value):
    level, own = 1.0, jax.random.fold_in(stream_key, 6)
    for axis_at, parts in pieces:
        steps = jnp.exp(jax.random.uniform(jax.random.fold_in(own, axis_at), (parts,), jnp.float32, least / len(pieces), top_value / len(pieces)))
        level = level * jnp.repeat(steps, dims[axis_at] // parts).reshape([-1 if axis == axis_at else 1 for axis in range(len(dims))])
    return level


def scatter_about(own_key, shape, width, bound, cuts=(), held_as=jnp.bfloat16):
    level = shard_levels(own_key, shape, cuts, -0.22, 0.18) if cuts else 1.0
    entries = jax.random.normal(own_key, shape, jnp.float32) * width * level
    return jnp.minimum(jnp.maximum(entries, -bound), bound).astype(held_as)


def setup_inputs(seed: int = 0, part: int = 0) -> dict:
    splits = jax.random.split(jax.random.key(seed), 11)
    part_splits = jax.random.split(jax.random.fold_in(splits[10], part), 11)
    controls = draw_controls(jax.random.fold_in(jax.random.fold_in(splits[10], part), 71), part)
    anomalies = scatter_about(part_splits[1], (2, K, GRID_ROW_EXTENT, GRID_COLUMN_SPAN), 1.0, 6.0, ((1, 2), (2, 4), (3, 2)))
    x_rates = draw_x_rates(jax.random.fold_in(jax.random.fold_in(splits[10], part), 71), part)
    y_rates = draw_y_rates(jax.random.fold_in(jax.random.fold_in(splits[10], part), 71), part)
    obs_cells = with_ends(jax.random.randint(part_splits[4], (N_GX, N_GY, OBS), 0, CX * CY), jax.random.fold_in(part_splits[4], 1), 0, (CX * CY) - 1).astype(jnp.int32)
    obs_codes = with_ends(jax.random.randint(part_splits[5], (N_GX, N_GY, OBS), 0, NDIR), jax.random.fold_in(part_splits[5], 1), 0, NDIR - 1).astype(jnp.int32)
    obs_values = scatter_about(part_splits[6], (N_GX, N_GY, OBS), 1.0, 6.0, ((0, 4), (1, 2)), jnp.float32)
    obs_weights = jnp.clip(jnp.exp(math.log(4.0) - 2.7725887 * jax.random.uniform(part_splits[7], (N_GX, N_GY, OBS), jnp.float32) ** shard_levels(part_splits[7], (N_GX, N_GY, OBS), ((0, 4), (1, 2)), -0.2, 0.2)), 0.25, 4.0)
    prev_gradient = draw_prev_gradient(jax.random.fold_in(jax.random.fold_in(splits[10], part), 71), part)
    prev_direction = scatter_about(part_splits[9], (K, GRID_ROW_EXTENT, GRID_COLUMN_SPAN), 1.0, 6.0, ((0, 2), (1, 4), (2, 2)), jnp.float32)
    return dict(controls=controls, anomalies=anomalies, x_rates=x_rates, y_rates=y_rates, obs_cells=obs_cells, obs_codes=obs_codes, obs_values=obs_values, obs_weights=obs_weights, prev_gradient=prev_gradient, prev_direction=prev_direction)


def recur(factor_field, weights, along_dim, reverse):
    factors = jnp.moveaxis(factor_field[None], along_dim, 0)
    shifted = jnp.moveaxis(weights, along_dim, 0)

    def advance(state, pair):
        factor, source = pair
        state = factor * state + source
        return (state, state)
    initial = jnp.zeros(shifted.shape[1:], shifted.dtype)
    _, states = lax.scan(advance, initial, (factors, shifted), reverse=reverse)
    return jnp.moveaxis(states, 0, along_dim)

def smooth(factor_field, gain_field, values, along_dim, adjoint):
    leading = factor_field * values if adjoint else gain_field * values
    inward = recur(factor_field, leading, along_dim, False)
    outward = recur(factor_field, gain_field * inward, along_dim, True)
    return gain_field / factor_field * outward if adjoint else outward

def reference(controls, anomalies, x_rates, y_rates, obs_cells, obs_codes, obs_values, obs_weights, prev_gradient, prev_direction):
    x_scales = jnp.sqrt(1.0 - x_rates * x_rates)
    y_scales = jnp.sqrt(1.0 - y_rates * y_rates)
    spread = 1.0 / math.sqrt(K - 1)
    filtered = smooth(y_rates, y_scales, smooth(x_rates, x_scales, controls, 1, False), 2, False)
    members = anomalies.astype(jnp.float32)
    increment = lax.optimization_barrier(jnp.sum(members * filtered[None], axis=1)) * spread
    tile_first = jnp.arange(N_GX, dtype=jnp.int32)[:, None, None]
    tile_second = jnp.arange(N_GY, dtype=jnp.int32)[None, :, None]
    cell_first = tile_first * CX + obs_cells // CY
    cell_second = tile_second * CY + obs_cells % CY
    bearing = obs_codes.astype(jnp.float32) * (2.0 * math.pi / NDIR)
    cosine = jnp.cos(bearing)
    sines = jnp.sin(bearing)
    projected = cosine * increment[0][cell_first, cell_second] + sines * increment[1][cell_first, cell_second]
    misfit = obs_weights * (projected - obs_values)
    back_east = jnp.zeros((GRID_ROW_EXTENT, GRID_COLUMN_SPAN), jnp.float32).at[cell_first, cell_second].add(cosine * misfit)
    back_north = jnp.zeros((GRID_ROW_EXTENT, GRID_COLUMN_SPAN), jnp.float32).at[cell_first, cell_second].add(sines * misfit)
    pulled = (members[0] * back_east[None] + members[1] * back_north[None]) * spread
    gradient = controls + smooth(x_rates, x_scales, smooth(y_rates, y_scales, pulled, 2, True), 1, True)
    numerator = jnp.sum(gradient * (gradient - prev_gradient))
    denominator = jnp.sum(prev_gradient * prev_gradient)
    direction = -gradient + numerator / denominator * prev_direction
    return (gradient, direction, increment)
```

```python
import functools
import math

import jax
import jax.numpy as jnp
from jax import lax
from jax.experimental import pallas as pl
from jax.experimental.pallas import tpu as pltpu
from jax.sharding import PartitionSpec as P

NDIR = 72
SUB = 8
LANES = 128
VMEM_SPEC = pl.BlockSpec(memory_space=pltpu.VMEM)


def call(body, out_shape, scratch=(), flops=100000, moved=100000):
    return pl.pallas_call(
        body,
        out_shape=out_shape,
        scratch_shapes=list(scratch),
        cost_estimate=pl.CostEstimate(flops=flops, bytes_accessed=moved, transcendentals=0),
    )


def f32(*shape):
    return jax.ShapeDtypeStruct(shape, jnp.float32)


def row_count(members):
    return -(-(members + 1) // SUB) * SUB


def chain(get, count, place):
    first = get(0)
    entering = jnp.zeros_like(first[0])
    if count == 1:
        return entering, entering
    for d in range(count - 1, 0, -1):
        out, _, product, _ = get(d)
        entering = jnp.where(place >= d, out + product * entering, entering)
    at = {}
    state = first[0] + first[2] * entering
    for d in range(1, count):
        at[d] = state
        if d < count - 1:
            out, _, product, _ = get(count - d)
            state = out + product * state
    backward = jnp.zeros_like(entering)
    for d in range(count - 1, 0, -1):
        _, out, product, response = get(count - d)
        backward = jnp.where(place + d < count, out + response * at[d] + product * backward, backward)
    return entering, backward


def source_reader(refs, count, axis):
    if len(refs) == count:
        return lambda d: refs[d][...]
    place = lax.axis_index(axis)
    return lambda d: refs[0][lax.rem(place - d + count, count)]


def x_reader(refs, count, axis, members):
    read = source_reader(refs, count, axis)
    half = row_count(members)

    def get(d):
        block = read(d)
        out, back = block[:half], block[half:]
        return out, back, out[members : members + 1], back[members : members + 1]

    return get


def y_reader(refs, count, axis, members):
    read = source_reader(refs, count, axis)
    half = LANES // 2

    def get(d):
        block = read(d)
        back = pltpu.roll(block, half, 1)
        return (
            block,
            back,
            jnp.broadcast_to(block[:, members : members + 1], block.shape),
            jnp.broadcast_to(back[:, members : members + 1], block.shape),
        )

    return get


def tables_of(rates, axis, reverse):
    width = rates.shape[axis]
    at = lax.broadcasted_iota(jnp.int32, rates.shape, axis)
    table = jnp.where(at == (width - 1 if reverse else 0), 0.0, rates)
    tables, step = [], 1
    while step < width:
        tables.append(table)
        table = table * pltpu.roll(table, width - step if reverse else step, axis)
        step *= 2
    return tables


def sweep(values, tables, axis, reverse):
    width = values.shape[axis]
    step = 1
    for table in tables:
        values = values + table * pltpu.roll(values, width - step if reverse else step, axis)
        step *= 2
    return values


def responses(rates, scales, axis, forward, reverse):
    at = lax.broadcasted_iota(jnp.int32, rates.shape, axis)
    product = sweep(jnp.where(at == 0, rates, 0.0), forward, axis, False)
    answer = sweep(scales * product, reverse, axis, True)
    behind = sweep(jnp.where(at == rates.shape[axis] - 1, rates, 0.0), reverse, axis, True)
    return product, answer, behind


def x_sweeps(get, count, rates, scales, store, message_ref):
    rows = rates.shape[0]
    half = row_count(count)
    forward, reverse = tables_of(rates, 0, False), tables_of(rates, 0, True)
    product, answer, behind = responses(rates, scales, 0, forward, reverse)
    store(count, answer)
    store(count + 1, behind)
    message_ref[count:half] = jnp.zeros((half - count, rates.shape[1]), jnp.float32)
    message_ref[half + count :] = jnp.zeros((half - count, rates.shape[1]), jnp.float32)
    message_ref[count : count + 1] = product[rows - 1 :]
    message_ref[half + count : half + count + 1] = answer[:1]
    for k in range(count):
        ahead = sweep(get(k), forward, 0, False)
        back = sweep(scales * ahead, reverse, 0, True)
        store(k, back)
        message_ref[k : k + 1] = ahead[rows - 1 :]
        message_ref[half + k : half + k + 1] = back[:1]


def y_sweeps(get, count, scales, forward, reverse, store, message_ref, products):
    rows, columns = scales.shape
    lane = lax.broadcasted_iota(jnp.int32, (rows, LANES), 1)
    half = LANES // 2
    message = jnp.where(lane == count, products[0], jnp.where(lane == half + count, products[1], 0.0))
    for k in range(count):
        ahead = sweep(get(k), forward, 1, False)
        back = sweep(scales * ahead, reverse, 1, True)
        store(k, back)
        message = jnp.where(lane == k, ahead[:, columns - 1 :], message)
        message = jnp.where(lane == half + k, back[:, :1], message)
    message_ref[...] = message


def split_dot(a, b, dims):
    rows = a.shape[0]
    high = a.astype(jnp.bfloat16)
    rest = a - high.astype(jnp.float32)
    middle = rest.astype(jnp.bfloat16)
    low = (rest - middle.astype(jnp.float32)).astype(jnp.bfloat16)
    parts = jnp.concatenate([high, middle, low], axis=0)
    out = lax.dot_general(parts, b, (dims, ((), ())), preferred_element_type=jnp.float32)
    return out[:rows] + (out[rows : 2 * rows] + out[2 * rows :])


def storer(ref):
    def store(k, value):
        ref[k] = value

    return store


def table_refs(ref):
    return [ref[n] for n in range(ref.shape[0])]


def first_kernel(members, controls_ref, rates_ref, local_ref, message_ref):
    rates = rates_ref[...]
    scales = jnp.sqrt(1.0 - rates * rates)
    x_sweeps(lambda k: scales * controls_ref[k], members, rates, scales, storer(local_ref), message_ref)


def tables_kernel(
    rates_ref, cells_ref, codes_ref, old_ref, forward_ref, reverse_ref, response_ref, columns_ref, weights_ref, old_sum_ref
):
    rates = rates_ref[...]
    rows, columns = rates.shape
    scales = jnp.sqrt(1.0 - rates * rates)
    forward, reverse = tables_of(rates, 1, False), tables_of(rates, 1, True)
    for n in range(len(forward)):
        forward_ref[n] = forward[n]
        reverse_ref[n] = reverse[n]
    for n, value in enumerate(responses(rates, scales, 1, forward, reverse)):
        response_ref[n] = value
    cells = cells_ref[...]
    count = cells.shape[1]
    at = lax.broadcasted_iota(jnp.int32, (columns, count), 0)
    columns_ref[...] = jnp.where(at == cells % columns, 1.0, 0.0).astype(jnp.bfloat16)
    bearing = codes_ref[...].astype(jnp.float32) * (2.0 * math.pi / NDIR)
    row = lax.broadcasted_iota(jnp.int32, (rows, count), 0) == cells // columns
    weights_ref[:rows] = jnp.where(row, jnp.cos(bearing), 0.0)
    weights_ref[rows:] = jnp.where(row, jnp.sin(bearing), 0.0)
    total = jnp.zeros((rows, columns), jnp.float32)
    for k in range(old_ref.shape[0]):
        total += old_ref[k] * old_ref[k]
    old_sum_ref[...] = total


def second_kernel(members, count, *refs):
    messages = refs[: -8]
    local_ref, rates_ref, forward_ref, reverse_ref, response_ref, out_ref, message_ref, states_ref = refs[-8:]
    rows, columns = rates_ref.shape
    place = lax.axis_index("gx")
    entering, backward = chain(x_reader(messages, count, "gx", members), count, place)
    half = row_count(members)
    states_ref[:half] = entering
    states_ref[half:] = backward
    y_rates = rates_ref[...]
    scales = jnp.sqrt(1.0 - y_rates * y_rates)
    ahead, behind = local_ref[members], local_ref[members + 1]

    def get(k):
        return scales * (local_ref[k] + ahead * states_ref[k : k + 1] + behind * states_ref[half + k : half + k + 1])

    products = (response_ref[0][:, columns - 1 :], response_ref[1][:, :1])
    forward, reverse = table_refs(forward_ref), table_refs(reverse_ref)
    y_sweeps(get, members, scales, forward, reverse, storer(out_ref), message_ref, products)


def third_kernel(members, count, spread, *refs):
    messages = refs[:-4]
    local_ref, response_ref, anomalies_ref, out_ref = refs[-4:]
    entering, backward = chain(y_reader(messages, count, "gy", members), count, lax.axis_index("gy"))
    ahead, behind = response_ref[1], response_ref[2]
    rows = ahead.shape[0]
    east, north = jnp.zeros_like(ahead), jnp.zeros_like(ahead)
    for k in range(members):
        filtered = local_ref[k] + ahead * entering[:, k : k + 1] + behind * backward[:, k : k + 1]
        east += anomalies_ref[0, k].astype(jnp.float32) * filtered
        north += anomalies_ref[1, k].astype(jnp.float32) * filtered
    out_ref[:rows] = east * spread
    out_ref[rows:] = north * spread


def fourth_kernel(members, spread, shares, *refs):
    partials = refs[:shares]
    (
        anomalies_ref,
        columns_ref,
        weights_ref,
        values_ref,
        precisions_ref,
        rates_ref,
        forward_ref,
        reverse_ref,
        response_ref,
        increment_ref,
        out_ref,
        message_ref,
    ) = refs[shares:]
    rates = rates_ref[...]
    rows, columns = rates.shape
    increment = partials[0][...]
    for ref in partials[1:]:
        increment = increment + ref[...]
    increment_ref[...] = increment
    picked = split_dot(increment, columns_ref[...], ((1,), (0,)))
    weights = weights_ref[...]
    projected = jnp.sum(weights * picked, axis=0, keepdims=True)
    misfit = precisions_ref[...] * (projected - values_ref[...])
    back = split_dot(weights * misfit, columns_ref[...], ((1,), (1,)))
    scales = jnp.sqrt(1.0 - rates * rates)
    east = back[:rows] * rates * spread
    north = back[rows:] * rates * spread

    def get(k):
        return anomalies_ref[0, k].astype(jnp.float32) * east + anomalies_ref[1, k].astype(jnp.float32) * north

    products = (response_ref[0][:, columns - 1 :], response_ref[1][:, :1])
    forward, reverse = table_refs(forward_ref), table_refs(reverse_ref)
    y_sweeps(get, members, scales, forward, reverse, storer(out_ref), message_ref, products)


def fifth_kernel(members, count, *refs):
    messages = refs[:-6]
    local_ref, response_ref, y_rates_ref, x_rates_ref, out_ref, message_ref = refs[-6:]
    entering, backward = chain(y_reader(messages, count, "gy", members), count, lax.axis_index("gy"))
    y_rates, x_rates = y_rates_ref[...], x_rates_ref[...]
    factor = x_rates * jnp.sqrt(1.0 - y_rates * y_rates) / y_rates
    ahead, behind = factor * response_ref[1], factor * response_ref[2]

    def get(k):
        return factor * local_ref[k] + ahead * entering[:, k : k + 1] + behind * backward[:, k : k + 1]

    x_sweeps(get, members, x_rates, jnp.sqrt(1.0 - x_rates * x_rates), storer(out_ref), message_ref)


def sixth_kernel(members, count, *refs):
    messages = refs[:-8]
    local_ref, rates_ref, controls_ref, old_ref, old_sum_ref, gradient_ref, sums_ref, states_ref = refs[-8:]
    entering, backward = chain(x_reader(messages, count, "gx", members), count, lax.axis_index("gx"))
    half = row_count(members)
    states_ref[:half] = entering
    states_ref[half:] = backward
    rates = rates_ref[...]
    rows, columns = rates.shape
    factor = jnp.sqrt(1.0 - rates * rates) / rates
    ahead, behind = factor * local_ref[members], factor * local_ref[members + 1]
    total = jnp.zeros((rows, columns), jnp.float32)
    for k in range(members):
        gradient = controls_ref[k] + (
            factor * local_ref[k] + ahead * states_ref[k : k + 1] + behind * states_ref[half + k : half + k + 1]
        )
        gradient_ref[k] = gradient
        total += gradient * (gradient - old_ref[k])
    sums_ref[:rows] = total
    sums_ref[rows:] = old_sum_ref[...]


def last_kernel(stacked, *refs):
    sums = refs[:-3]
    gradient_ref, old_ref, direction_ref = refs[-3:]
    if stacked:
        total = jnp.sum(sums[0][...], axis=0)
    else:
        total = sums[0][...]
        for ref in sums[1:]:
            total = total + ref[...]
    half = total.shape[0] // 2
    numerator = jnp.sum(total[:half], axis=(0, 1), keepdims=True)
    denominator = jnp.sum(total[half:], axis=(0, 1), keepdims=True)
    ratio = numerator / denominator
    for k in range(gradient_ref.shape[0]):
        direction_ref[k] = ratio * old_ref[k] - gradient_ref[k]


def exchange(message, axis, count):
    if count <= 4:
        shifts = range(1, count)
        return [message] + [lax.ppermute(message, axis, [(i, (i + d) % count) for i in range(count)]) for d in shifts]
    return [lax.all_gather(message, axis)]


def add_over(values, axis, count):
    if count == 2:
        return values + lax.ppermute(values, axis, [(0, 1), (1, 0)])
    return lax.psum(values, axis)


def shards(
    n_gx,
    n_gy,
    n_gz,
    controls,
    anomalies,
    x_rates,
    y_rates,
    obs_cells,
    obs_codes,
    obs_values,
    obs_weights,
    prev_gradient,
    prev_direction,
):
    members, rows, columns = controls.shape
    spread = 1.0 / math.sqrt(members * n_gz - 1)
    lines = 2 * row_count(members)
    observed = obs_cells.size
    depth = (columns - 1).bit_length()
    field = (members, rows, columns)
    extended = (members + 2, rows, columns)

    local, message = call(
        functools.partial(first_kernel, members), (f32(*extended), f32(lines, columns))
    )(controls, x_rates)
    x_messages = exchange(message, "gx", n_gx)
    forward, reverse, response, column_ones, row_weights, old_sum = call(
        tables_kernel,
        (
            f32(depth, rows, columns),
            f32(depth, rows, columns),
            f32(3, rows, columns),
            jax.ShapeDtypeStruct((columns, observed), jnp.bfloat16),
            f32(2 * rows, observed),
            f32(rows, columns),
        ),
    )(y_rates, obs_cells.reshape(1, observed), obs_codes.reshape(1, observed), prev_gradient)
    filtered, message = call(
        functools.partial(second_kernel, members, n_gx),
        (f32(*field), f32(rows, LANES)),
        [pltpu.VMEM((lines, columns), jnp.float32)],
    )(*x_messages, local, y_rates, forward, reverse, response)
    partial = call(functools.partial(third_kernel, members, n_gy, spread), f32(2 * rows, columns))(
        *exchange(message, "gy", n_gy), filtered, response, anomalies
    )
    if n_gz == 2:
        partials = [partial, lax.ppermute(partial, "gz", [(0, 1), (1, 0)])]
    else:
        partials = [lax.psum(partial, "gz")]
    increment, pulled, message = call(
        functools.partial(fourth_kernel, members, spread, len(partials)),
        (f32(2 * rows, columns), f32(*field), f32(rows, LANES)),
    )(
        *partials,
        anomalies,
        column_ones,
        row_weights,
        obs_values.reshape(1, observed),
        obs_weights.reshape(1, observed),
        y_rates,
        forward,
        reverse,
        response,
    )
    local, message = call(
        functools.partial(fifth_kernel, members, n_gy),
        (f32(*extended), f32(lines, columns)),
    )(*exchange(message, "gy", n_gy), pulled, response, y_rates, x_rates)
    gradient, sums = call(
        functools.partial(sixth_kernel, members, n_gx),
        (f32(*field), f32(2 * rows, columns)),
        [pltpu.VMEM((lines, columns), jnp.float32)],
    )(*exchange(message, "gx", n_gx), local, x_rates, controls, prev_gradient, old_sum)
    sums = add_over(add_over(sums, "gz", n_gz), "gy", n_gy)
    totals = exchange(sums, "gx", n_gx)
    direction = call(functools.partial(last_kernel, len(totals) != n_gx), f32(*field))(
        *totals, gradient, prev_direction
    )
    return gradient, direction, increment.reshape(2, rows, columns)


def solution(mesh):
    in_specs = (
        P("gz", ("grp", "gx"), "gy"),
        P(None, "gz", ("grp", "gx"), "gy"),
        P(("grp", "gx"), "gy"),
        P(("grp", "gx"), "gy"),
        P(("grp", "gx"), "gy", None),
        P(("grp", "gx"), "gy", None),
        P(("grp", "gx"), "gy", None),
        P(("grp", "gx"), "gy", None),
        P("gz", ("grp", "gx"), "gy"),
        P("gz", ("grp", "gx"), "gy"),
    )
    out_specs = (
        P("gz", ("grp", "gx"), "gy"),
        P("gz", ("grp", "gx"), "gy"),
        P(None, ("grp", "gx"), "gy"),
    )
    body = functools.partial(shards, mesh.shape["gx"], mesh.shape["gy"], mesh.shape["gz"])
    return jax.shard_map(body, mesh=mesh, in_specs=in_specs, out_specs=out_specs, check_vma=False)
```

```python
import functools
import math

import jax
import jax.numpy as jnp
from jax import lax
from jax.experimental import pallas as pl
from jax.experimental.pallas import tpu as pltpu
from jax.sharding import PartitionSpec as P

NDIR = 72
SUB = 8
LANES = 128
LIMIT = 8 * 2**20
VMEM_SPEC = pl.BlockSpec(memory_space=pltpu.VMEM)
HBM_SPEC = pl.BlockSpec(memory_space=pltpu.HBM)


def call(body, out_shape, scratch=(), flops=100000, moved=100000, **specs):
    return pl.pallas_call(
        body,
        out_shape=out_shape,
        **specs,
        compiler_params=pltpu.CompilerParams(vmem_limit_bytes=LIMIT),
        scratch_shapes=list(scratch),
        cost_estimate=pl.CostEstimate(flops=flops, bytes_accessed=moved, transcendentals=0),
    )


def f32(*shape):
    return jax.ShapeDtypeStruct(shape, jnp.float32)


def row_count(members):
    return -(-(members + 1) // SUB) * SUB


def chain(get, count, place):
    first = get(0)
    entering = jnp.zeros_like(first[0])
    if count == 1:
        return entering, entering
    for d in range(count - 1, 0, -1):
        out, _, product, _ = get(d)
        entering = jnp.where(place >= d, out + product * entering, entering)
    at = {}
    state = first[0] + first[2] * entering
    for d in range(1, count):
        at[d] = state
        if d < count - 1:
            out, _, product, _ = get(count - d)
            state = out + product * state
    backward = jnp.zeros_like(entering)
    for d in range(count - 1, 0, -1):
        _, out, product, response = get(count - d)
        backward = jnp.where(place + d < count, out + response * at[d] + product * backward, backward)
    return entering, backward


def source_reader(refs, count, axis):
    if len(refs) == count:
        return lambda d: refs[d][...]
    place = lax.axis_index(axis)
    return lambda d: refs[0][lax.rem(place - d + count, count)]


def x_reader(refs, count, axis, members):
    read = source_reader(refs, count, axis)
    half = row_count(members)

    def get(d):
        block = read(d)
        out, back = block[:half], block[half:]
        return out, back, out[members : members + 1], back[members : members + 1]

    return get


def y_reader(refs, count, axis, members):
    read = source_reader(refs, count, axis)
    half = LANES // 2

    def get(d):
        block = read(d)
        back = pltpu.roll(block, half, 1)
        return (
            block,
            back,
            jnp.broadcast_to(block[:, members : members + 1], block.shape),
            jnp.broadcast_to(back[:, members : members + 1], block.shape),
        )

    return get


def tables_of(rates, axis, reverse):
    width = rates.shape[axis]
    at = lax.broadcasted_iota(jnp.int32, rates.shape, axis)
    table = jnp.where(at == (width - 1 if reverse else 0), 0.0, rates)
    tables, step = [], 1
    while step < width:
        tables.append(table)
        table = table * pltpu.roll(table, width - step if reverse else step, axis)
        step *= 2
    return tables


def sweep(values, tables, axis, reverse):
    width = values.shape[axis]
    step = 1
    for table in tables:
        values = values + table * pltpu.roll(values, width - step if reverse else step, axis)
        step *= 2
    return values


def responses(rates, scales, axis, forward, reverse):
    at = lax.broadcasted_iota(jnp.int32, rates.shape, axis)
    product = sweep(jnp.where(at == 0, rates, 0.0), forward, axis, False)
    answer = sweep(scales * product, reverse, axis, True)
    behind = sweep(jnp.where(at == rates.shape[axis] - 1, rates, 0.0), reverse, axis, True)
    return product, answer, behind


def x_sweeps(get, count, rates, scales, store, message_ref):
    rows = rates.shape[0]
    half = row_count(count)
    forward, reverse = tables_of(rates, 0, False), tables_of(rates, 0, True)
    product, answer, behind = responses(rates, scales, 0, forward, reverse)
    store(count, answer)
    store(count + 1, behind)
    message_ref[count:half] = jnp.zeros((half - count, rates.shape[1]), jnp.float32)
    message_ref[half + count :] = jnp.zeros((half - count, rates.shape[1]), jnp.float32)
    message_ref[count : count + 1] = product[rows - 1 :]
    message_ref[half + count : half + count + 1] = answer[:1]
    for k in range(count):
        ahead = sweep(get(k), forward, 0, False)
        back = sweep(scales * ahead, reverse, 0, True)
        store(k, back)
        message_ref[k : k + 1] = ahead[rows - 1 :]
        message_ref[half + k : half + k + 1] = back[:1]


def y_sweeps(get, count, scales, forward, reverse, store, message_ref, products):
    rows, columns = scales.shape
    lane = lax.broadcasted_iota(jnp.int32, (rows, LANES), 1)
    half = LANES // 2
    message = jnp.where(lane == count, products[0], jnp.where(lane == half + count, products[1], 0.0))
    for k in range(count):
        ahead = sweep(get(k), forward, 1, False)
        back = sweep(scales * ahead, reverse, 1, True)
        store(k, back)
        message = jnp.where(lane == k, ahead[:, columns - 1 :], message)
        message = jnp.where(lane == half + k, back[:, :1], message)
    message_ref[...] = message


def split_dot(a, b, dims):
    rows = a.shape[0]
    high = a.astype(jnp.bfloat16)
    rest = a - high.astype(jnp.float32)
    middle = rest.astype(jnp.bfloat16)
    low = (rest - middle.astype(jnp.float32)).astype(jnp.bfloat16)
    parts = jnp.concatenate([high, middle, low], axis=0)
    out = lax.dot_general(parts, b, (dims, ((), ())), preferred_element_type=jnp.float32)
    return out[:rows] + (out[rows : 2 * rows] + out[2 * rows :])


def storer(ref):
    def store(k, value):
        ref[k] = value

    return store


def table_refs(ref):
    return [ref[n] for n in range(ref.shape[0])]


def first_kernel(members, far_controls_ref, far_rates_ref, local_ref, message_ref, controls_ref, rates_ref, semaphores):
    fetches = (
        pltpu.make_async_copy(far_rates_ref, rates_ref, semaphores.at[0]),
        pltpu.make_async_copy(far_controls_ref, controls_ref, semaphores.at[1]),
    )
    for fetch in fetches:
        fetch.start()
    for fetch in fetches:
        fetch.wait()
    rates = rates_ref[...]
    scales = jnp.sqrt(1.0 - rates * rates)
    x_sweeps(lambda k: scales * controls_ref[k], members, rates, scales, storer(local_ref), message_ref)


def tables_kernel(
    rates_ref,
    cells_ref,
    codes_ref,
    values_ref,
    precisions_ref,
    old_ref,
    forward_ref,
    reverse_ref,
    response_ref,
    columns_ref,
    weights_ref,
    old_sum_ref,
):
    rates = rates_ref[...]
    rows, columns = rates.shape
    scales = jnp.sqrt(1.0 - rates * rates)
    forward, reverse = tables_of(rates, 1, False), tables_of(rates, 1, True)
    for n in range(len(forward)):
        forward_ref[n] = forward[n]
        reverse_ref[n] = reverse[n]
    for n, value in enumerate(responses(rates, scales, 1, forward, reverse)):
        response_ref[n] = value
    cells = cells_ref[...]
    count = cells.shape[1]
    at = lax.broadcasted_iota(jnp.int32, (columns, count), 0)
    columns_ref[...] = jnp.where(at == cells % columns, 1.0, 0.0).astype(jnp.bfloat16)
    bearing = codes_ref[...].astype(jnp.float32) * (2.0 * math.pi / NDIR)
    row = lax.broadcasted_iota(jnp.int32, (rows, count), 0) == cells // columns
    weights_ref[:rows] = jnp.where(row, jnp.cos(bearing), 0.0)
    weights_ref[rows : 2 * rows] = jnp.where(row, jnp.sin(bearing), 0.0)
    weights_ref[2 * rows : 2 * rows + 1] = values_ref[...]
    weights_ref[2 * rows + 1 : 2 * rows + 2] = precisions_ref[...]
    total = jnp.zeros((rows, columns), jnp.float32)
    for k in range(old_ref.shape[0]):
        total += old_ref[k] * old_ref[k]
    old_sum_ref[...] = total


def second_kernel(members, count, *refs):
    messages = refs[: -8]
    local_ref, rates_ref, forward_ref, reverse_ref, response_ref, out_ref, message_ref, states_ref = refs[-8:]
    rows, columns = rates_ref.shape
    place = lax.axis_index("gx")
    entering, backward = chain(x_reader(messages, count, "gx", members), count, place)
    half = row_count(members)
    states_ref[:half] = entering
    states_ref[half:] = backward
    y_rates = rates_ref[...]
    scales = jnp.sqrt(1.0 - y_rates * y_rates)
    ahead, behind = local_ref[members], local_ref[members + 1]

    def get(k):
        return scales * (local_ref[k] + ahead * states_ref[k : k + 1] + behind * states_ref[half + k : half + k + 1])

    products = (response_ref[0][:, columns - 1 :], response_ref[1][:, :1])
    forward, reverse = table_refs(forward_ref), table_refs(reverse_ref)
    y_sweeps(get, members, scales, forward, reverse, storer(out_ref), message_ref, products)


def third_kernel(members, count, spread, *refs):
    messages = refs[:-4]
    local_ref, response_ref, anomalies_ref, out_ref = refs[-4:]
    entering, backward = chain(y_reader(messages, count, "gy", members), count, lax.axis_index("gy"))
    ahead, behind = response_ref[1], response_ref[2]
    rows = ahead.shape[0]
    east, north = jnp.zeros_like(ahead), jnp.zeros_like(ahead)
    for k in range(members):
        filtered = local_ref[k] + ahead * entering[:, k : k + 1] + behind * backward[:, k : k + 1]
        east += anomalies_ref[0, k].astype(jnp.float32) * filtered
        north += anomalies_ref[1, k].astype(jnp.float32) * filtered
    out_ref[:rows] = east * spread
    out_ref[rows:] = north * spread


def fourth_kernel(members, spread, shares, *refs):
    partials = refs[:shares]
    (
        anomalies_ref,
        columns_ref,
        weights_ref,
        rates_ref,
        forward_ref,
        reverse_ref,
        response_ref,
        increment_ref,
        out_ref,
        message_ref,
    ) = refs[shares:]
    rates = rates_ref[...]
    rows, columns = rates.shape
    increment = partials[0][...]
    for ref in partials[1:]:
        increment = increment + ref[...]
    increment_ref[...] = increment
    picked = split_dot(increment, columns_ref[...], ((1,), (0,)))
    weights = weights_ref[: 2 * rows]
    values, precisions = weights_ref[2 * rows : 2 * rows + 1], weights_ref[2 * rows + 1 : 2 * rows + 2]
    projected = jnp.sum(weights * picked, axis=0, keepdims=True)
    misfit = precisions * (projected - values)
    back = split_dot(weights * misfit, columns_ref[...], ((1,), (1,)))
    scales = jnp.sqrt(1.0 - rates * rates)
    east = back[:rows] * rates * spread
    north = back[rows:] * rates * spread

    def get(k):
        return anomalies_ref[0, k].astype(jnp.float32) * east + anomalies_ref[1, k].astype(jnp.float32) * north

    products = (response_ref[0][:, columns - 1 :], response_ref[1][:, :1])
    forward, reverse = table_refs(forward_ref), table_refs(reverse_ref)
    y_sweeps(get, members, scales, forward, reverse, storer(out_ref), message_ref, products)


def fifth_kernel(members, count, *refs):
    messages = refs[:-6]
    local_ref, response_ref, y_rates_ref, x_rates_ref, out_ref, message_ref = refs[-6:]
    entering, backward = chain(y_reader(messages, count, "gy", members), count, lax.axis_index("gy"))
    y_rates, x_rates = y_rates_ref[...], x_rates_ref[...]
    factor = x_rates * jnp.sqrt(1.0 - y_rates * y_rates) / y_rates
    ahead, behind = factor * response_ref[1], factor * response_ref[2]

    def get(k):
        return factor * local_ref[k] + ahead * entering[:, k : k + 1] + behind * backward[:, k : k + 1]

    x_sweeps(get, members, x_rates, jnp.sqrt(1.0 - x_rates * x_rates), storer(out_ref), message_ref)


def sixth_kernel(members, count, *refs):
    messages = refs[:-8]
    local_ref, rates_ref, controls_ref, old_ref, old_sum_ref, gradient_ref, sums_ref, states_ref = refs[-8:]
    entering, backward = chain(x_reader(messages, count, "gx", members), count, lax.axis_index("gx"))
    half = row_count(members)
    states_ref[:half] = entering
    states_ref[half:] = backward
    rates = rates_ref[...]
    rows, columns = rates.shape
    factor = jnp.sqrt(1.0 - rates * rates) / rates
    ahead, behind = factor * local_ref[members], factor * local_ref[members + 1]
    total = jnp.zeros((rows, columns), jnp.float32)
    for k in range(members):
        gradient = controls_ref[k] + (
            factor * local_ref[k] + ahead * states_ref[k : k + 1] + behind * states_ref[half + k : half + k + 1]
        )
        gradient_ref[k] = gradient
        total += gradient * (gradient - old_ref[k])
    sums = (jnp.sum(total, axis=0, keepdims=True), jnp.sum(old_sum_ref[...], axis=0, keepdims=True))
    row = lax.broadcasted_iota(jnp.int32, (SUB, columns), 0)
    sums = jnp.where(row == 0, sums[0], jnp.where(row == 1, sums[1], 0.0))
    packed = sums[:, :LANES]
    for at in range(LANES, columns, LANES):
        packed = packed + sums[:, at : at + LANES]
    for n in range(sums_ref.shape[0]):
        sums_ref[n] = packed


def last_kernel(sums_ref, near_ref, old_ref, gradient_ref, far_ref, direction_ref, semaphores):
    copies = [pltpu.make_async_copy(near_ref, gradient_ref, semaphores.at[0])]
    copies[0].start()
    total = jnp.sum(sums_ref[...], axis=0)
    numerator = jnp.sum(total[:1], axis=1, keepdims=True)
    denominator = jnp.sum(total[1:2], axis=1, keepdims=True)
    ratio = numerator / denominator
    for k in range(near_ref.shape[0]):
        direction_ref[k] = ratio * old_ref[k] - near_ref[k]
    copies.append(pltpu.make_async_copy(direction_ref, far_ref, semaphores.at[1]))
    copies[1].start()
    for copy in copies:
        copy.wait()


def exchange(message, axis, count):
    if count <= 4:
        shifts = range(1, count)
        return [message] + [lax.ppermute(message, axis, [(i, (i + d) % count) for i in range(count)]) for d in shifts]
    return [lax.all_gather(message, axis)]


def shards(
    n_gx,
    n_gy,
    n_gz,
    controls,
    anomalies,
    x_rates,
    y_rates,
    obs_cells,
    obs_codes,
    obs_values,
    obs_weights,
    prev_gradient,
    prev_direction,
):
    members, rows, columns = controls.shape
    spread = 1.0 / math.sqrt(members * n_gz - 1)
    lines = 2 * row_count(members)
    observed = obs_cells.size
    depth = (columns - 1).bit_length()
    field = (members, rows, columns)
    extended = (members + 2, rows, columns)

    local, message = call(
        functools.partial(first_kernel, members), (f32(*extended), f32(lines, columns)),
        [pltpu.VMEM(field, jnp.float32), pltpu.VMEM((rows, columns), jnp.float32), pltpu.SemaphoreType.DMA((2,))],
        in_specs=[HBM_SPEC, HBM_SPEC],
    )(controls, x_rates)
    x_messages = exchange(message, "gx", n_gx)
    forward, reverse, response, column_ones, row_weights, old_sum = call(
        tables_kernel,
        (
            f32(depth, rows, columns),
            f32(depth, rows, columns),
            f32(3, rows, columns),
            jax.ShapeDtypeStruct((columns, observed), jnp.bfloat16),
            f32(2 * rows + SUB, observed),
            f32(rows, columns),
        ),
    )(
        y_rates,
        obs_cells.reshape(1, observed),
        obs_codes.reshape(1, observed),
        obs_values.reshape(1, observed),
        obs_weights.reshape(1, observed),
        prev_gradient,
    )
    filtered, message = call(
        functools.partial(second_kernel, members, n_gx),
        (f32(*field), f32(rows, LANES)),
        [pltpu.VMEM((lines, columns), jnp.float32)],
    )(*x_messages, local, y_rates, forward, reverse, response)
    partial = call(functools.partial(third_kernel, members, n_gy, spread), f32(2 * rows, columns))(
        *exchange(message, "gy", n_gy), filtered, response, anomalies
    )
    if n_gz == 2:
        partials = [partial, lax.ppermute(partial, "gz", [(0, 1), (1, 0)])]
    else:
        partials = [lax.psum(partial, "gz")]
    increment, pulled, message = call(
        functools.partial(fourth_kernel, members, spread, len(partials)),
        (f32(2 * rows, columns), f32(*field), f32(rows, LANES)),
    )(
        *partials,
        anomalies,
        column_ones,
        row_weights,
        y_rates,
        forward,
        reverse,
        response,
    )
    local, message = call(
        functools.partial(fifth_kernel, members, n_gy),
        (f32(*extended), f32(lines, columns)),
    )(*exchange(message, "gy", n_gy), pulled, response, y_rates, x_rates)
    gradient, sums = call(
        functools.partial(sixth_kernel, members, n_gx),
        (f32(*field), f32(n_gx * n_gy * n_gz, SUB, LANES)),
        [pltpu.VMEM((lines, columns), jnp.float32)],
    )(*exchange(message, "gx", n_gx), local, x_rates, controls, prev_gradient, old_sum)
    sums = lax.all_to_all(sums, ("gx", "gy", "gz"), 0, 0)
    gradient, direction = call(
        last_kernel,
        (f32(*field), f32(*field)),
        [pltpu.VMEM(field, jnp.float32), pltpu.SemaphoreType.DMA((2,))],
        out_specs=(HBM_SPEC, HBM_SPEC),
    )(sums, gradient, prev_direction)
    return gradient, direction, increment.reshape(2, rows, columns)


def solution(mesh):
    in_specs = (
        P("gz", ("grp", "gx"), "gy"),
        P(None, "gz", ("grp", "gx"), "gy"),
        P(("grp", "gx"), "gy"),
        P(("grp", "gx"), "gy"),
        P(("grp", "gx"), "gy", None),
        P(("grp", "gx"), "gy", None),
        P(("grp", "gx"), "gy", None),
        P(("grp", "gx"), "gy", None),
        P("gz", ("grp", "gx"), "gy"),
        P("gz", ("grp", "gx"), "gy"),
    )
    out_specs = (
        P("gz", ("grp", "gx"), "gy"),
        P("gz", ("grp", "gx"), "gy"),
        P(None, ("grp", "gx"), "gy"),
    )
    body = functools.partial(shards, mesh.shape["gx"], mesh.shape["gy"], mesh.shape["gz"])
    return jax.shard_map(body, mesh=mesh, in_specs=in_specs, out_specs=out_specs, check_vma=False)
```

```python
import functools
import math

import jax
import jax.numpy as jnp
from jax import lax
from jax.experimental import pallas as pl
from jax.experimental.pallas import tpu as pltpu
from jax.sharding import PartitionSpec as P

NDIR = 72
SUB = 8
LANES = 128
LIMIT = 8 * 2**20
VMEM_SPEC = pl.BlockSpec(memory_space=pltpu.VMEM)
HBM_SPEC = pl.BlockSpec(memory_space=pltpu.HBM)


def call(body, out_shape, scratch=(), flops=100000, moved=100000, **specs):
    return pl.pallas_call(
        body,
        out_shape=out_shape,
        **specs,
        compiler_params=pltpu.CompilerParams(vmem_limit_bytes=LIMIT),
        scratch_shapes=list(scratch),
        cost_estimate=pl.CostEstimate(flops=flops, bytes_accessed=moved, transcendentals=0),
    )


def f32(*shape):
    return jax.ShapeDtypeStruct(shape, jnp.float32)


def row_count(members):
    return -(-(members + 4) // SUB) * SUB


def chain(get, count, place, everywhere=False):
    first = get(0)
    zero = jnp.zeros_like(first[0])
    if count == 1:
        return zero, zero, [(zero, zero)]
    low, high, low_back, high_back = {}, {}, {}, {}
    state = zero
    for d in range(count - 1, 0, -1):
        low[d] = state
        out, _, product, _ = get(d)
        state = jnp.where(place >= d, out + product * state, state)
    entering = state
    state = first[0] + first[2] * entering
    for d in range(1, count):
        high[d] = state
        if d < count - 1:
            out, _, product, _ = get(count - d)
            state = out + product * state
    state = zero
    for d in range(count - 1, 0, -1):
        high_back[d] = state
        _, out, product, response = get(count - d)
        state = jnp.where(place + d < count, out + response * high[d] + product * state, state)
    backward = state
    if not everywhere:
        return entering, backward, []
    state = first[1] + first[3] * entering + first[2] * backward
    for d in range(1, count):
        low_back[d] = state
        if d < count - 1:
            _, out, product, response = get(d)
            state = out + response * low[d] + product * state
    every = [(entering, backward)]
    for d in range(1, count):
        above = count - d
        every.append(
            (
                jnp.where(place >= d, low[d], high[above]),
                jnp.where(place >= d, low_back[d], high_back[above]),
            )
        )
    return entering, backward, every


def source_reader(refs, count, axis):
    if len(refs) == count:
        return lambda d: refs[d][...]
    place = lax.axis_index(axis)
    return lambda d: refs[0][lax.rem(place - d + count, count)]


def x_reader(refs, count, axis, members):
    read = source_reader(refs, count, axis)
    half = row_count(members)

    def get(d):
        block = read(d)
        out, back = block[:half], block[half:]
        return out, back, out[members : members + 1], back[members : members + 1]

    return get


def y_reader(refs, count, axis, members):
    read = source_reader(refs, count, axis)
    half = LANES // 2

    def get(d):
        block = read(d)
        back = pltpu.roll(block, half, 1)
        return (
            block,
            back,
            jnp.broadcast_to(block[:, members : members + 1], block.shape),
            jnp.broadcast_to(back[:, members : members + 1], block.shape),
        )

    return get


def tables_of(rates, axis, reverse):
    width = rates.shape[axis]
    at = lax.broadcasted_iota(jnp.int32, rates.shape, axis)
    table = jnp.where(at == (width - 1 if reverse else 0), 0.0, rates)
    tables, step = [], 1
    while step < width:
        tables.append(table)
        table = table * pltpu.roll(table, width - step if reverse else step, axis)
        step *= 2
    return tables


def sweep(values, tables, axis, reverse):
    width = values.shape[axis]
    step = 1
    for table in tables:
        values = values + table * pltpu.roll(values, width - step if reverse else step, axis)
        step *= 2
    return values


def responses(rates, scales, axis, forward, reverse):
    at = lax.broadcasted_iota(jnp.int32, rates.shape, axis)
    product = sweep(jnp.where(at == 0, rates, 0.0), forward, axis, False)
    answer = sweep(scales * product, reverse, axis, True)
    behind = sweep(jnp.where(at == rates.shape[axis] - 1, rates, 0.0), reverse, axis, True)
    return product, answer, behind


def x_sweeps(get, count, rates, scales, take):
    forward, reverse = tables_of(rates, 0, False), tables_of(rates, 0, True)
    for k in range(count):
        ahead = sweep(get(k), forward, 0, False)
        take(k, ahead, sweep(scales * ahead, reverse, 0, True))


def send_y(get, count, response_ref, message_ref):
    last, first = response_ref[3], response_ref[4]
    rows, columns = last.shape
    lane = lax.broadcasted_iota(jnp.int32, (rows, LANES), 1)
    half = LANES // 2
    product, answer = response_ref[0][:, columns - 1 :], response_ref[1][:, :1]
    message = jnp.where(lane == count, product, jnp.where(lane == half + count, answer, 0.0))
    for k in range(count):
        weights = get(k)
        message = jnp.where(lane == k, jnp.sum(last * weights, axis=1, keepdims=True), message)
        message = jnp.where(lane == half + k, jnp.sum(first * weights, axis=1, keepdims=True), message)
    message_ref[...] = message


def split_dot(a, b, dims):
    rows = a.shape[0]
    high = a.astype(jnp.bfloat16)
    rest = a - high.astype(jnp.float32)
    middle = rest.astype(jnp.bfloat16)
    low = (rest - middle.astype(jnp.float32)).astype(jnp.bfloat16)
    parts = jnp.concatenate([high, middle, low], axis=0)
    out = lax.dot_general(parts, b, (dims, ((), ())), preferred_element_type=jnp.float32)
    return out[:rows] + (out[rows : 2 * rows] + out[2 * rows :])


def first_kernel(members, far_controls_ref, far_rates_ref, local_ref, message_ref, controls_ref, rates_ref, semaphores):
    fetches = (
        pltpu.make_async_copy(far_rates_ref, rates_ref, semaphores.at[0]),
        pltpu.make_async_copy(far_controls_ref, controls_ref, semaphores.at[1]),
    )
    for fetch in fetches:
        fetch.start()
    for fetch in fetches:
        fetch.wait()
    rates = rates_ref[...]
    rows, columns = rates.shape
    scales = jnp.sqrt(1.0 - rates * rates)
    half = row_count(members)
    forward, reverse = tables_of(rates, 0, False), tables_of(rates, 0, True)
    product, answer, behind = responses(rates, scales, 0, forward, reverse)
    local_ref[members] = answer
    local_ref[members + 1] = behind
    factor = scales / rates
    ahead, behind = factor * answer, factor * behind
    message_ref[members:half] = jnp.zeros((half - members, columns), jnp.float32)
    message_ref[half + members :] = jnp.zeros((half - members, columns), jnp.float32)
    message_ref[members : members + 1] = product[rows - 1 :]
    message_ref[members + 1 : members + 2] = jnp.sum(ahead * ahead, axis=0, keepdims=True)
    message_ref[members + 2 : members + 3] = jnp.sum(2.0 * ahead * behind, axis=0, keepdims=True)
    message_ref[members + 3 : members + 4] = jnp.sum(behind * behind, axis=0, keepdims=True)
    message_ref[half + members : half + members + 1] = answer[:1]

    def take(k, ahead, back):
        local_ref[k] = back
        message_ref[k : k + 1] = ahead[rows - 1 :]
        message_ref[half + k : half + k + 1] = back[:1]

    x_sweeps(lambda k: scales * controls_ref[k], members, rates, scales, take)


def tables_kernel(
    rates_ref,
    cells_ref,
    codes_ref,
    values_ref,
    precisions_ref,
    old_ref,
    forward_ref,
    reverse_ref,
    response_ref,
    columns_ref,
    weights_ref,
    old_sum_ref,
):
    rates = rates_ref[...]
    rows, columns = rates.shape
    scales = jnp.sqrt(1.0 - rates * rates)
    forward, reverse = tables_of(rates, 1, False), tables_of(rates, 1, True)
    for n in range(len(forward)):
        forward_ref[n] = forward[n]
        reverse_ref[n] = reverse[n]
    product, answer, behind = responses(rates, scales, 1, forward, reverse)
    lane = lax.broadcasted_iota(jnp.int32, rates.shape, 1)
    response_ref[0] = product
    response_ref[1] = answer
    response_ref[2] = behind
    response_ref[3] = jnp.where(lane == columns - 1, 1.0, pltpu.roll(behind, columns - 1, 1))
    reach = scales * jnp.where(lane == 0, 1.0, pltpu.roll(product, 1, 1))
    carried = sweep(rates * reach, reverse, 1, True)
    response_ref[4] = reach + jnp.where(lane == columns - 1, 0.0, pltpu.roll(carried, columns - 1, 1))
    cells = cells_ref[...]
    count = cells.shape[1]
    at = lax.broadcasted_iota(jnp.int32, (columns, count), 0)
    columns_ref[...] = jnp.where(at == cells % columns, 1.0, 0.0).astype(jnp.bfloat16)
    bearing = codes_ref[...].astype(jnp.float32) * (2.0 * math.pi / NDIR)
    row = lax.broadcasted_iota(jnp.int32, (rows, count), 0) == cells // columns
    weights_ref[:rows] = jnp.where(row, jnp.cos(bearing), 0.0)
    weights_ref[rows : 2 * rows] = jnp.where(row, jnp.sin(bearing), 0.0)
    weights_ref[2 * rows : 2 * rows + 1] = values_ref[...]
    weights_ref[2 * rows + 1 : 2 * rows + 2] = precisions_ref[...]
    total = jnp.zeros((rows, columns), jnp.float32)
    for k in range(old_ref.shape[0]):
        total += old_ref[k] * old_ref[k]
    old_sum_ref[...] = total


def second_kernel(members, count, *refs):
    messages = refs[:-6]
    local_ref, rates_ref, response_ref, out_ref, message_ref, states_ref = refs[-6:]
    place = lax.axis_index("gx")
    entering, backward, _ = chain(x_reader(messages, count, "gx", members), count, place)
    half = row_count(members)
    states_ref[:half] = entering
    states_ref[half:] = backward
    rates = rates_ref[...]
    scales = jnp.sqrt(1.0 - rates * rates)
    local, ahead, behind = scales, scales * local_ref[members], scales * local_ref[members + 1]

    def get(k):
        weights = (
            local * local_ref[k] + ahead * states_ref[k : k + 1] + behind * states_ref[half + k : half + k + 1]
        )
        out_ref[k] = weights
        return weights

    send_y(get, members, response_ref, message_ref)


def sweep_kernel(weights_ref, rates_ref, forward_ref, reverse_ref, out_ref):
    rates = rates_ref[...]
    scales = jnp.sqrt(1.0 - rates * rates)
    forward = [forward_ref[n] for n in range(forward_ref.shape[0])]
    reverse = [reverse_ref[n] for n in range(reverse_ref.shape[0])]
    for k in range(weights_ref.shape[0]):
        out_ref[k] = sweep(scales * sweep(weights_ref[k], forward, 1, False), reverse, 1, True)


def third_kernel(members, count, spread, *refs):
    messages = refs[:-4]
    local_ref, response_ref, anomalies_ref, out_ref = refs[-4:]
    entering, backward, _ = chain(y_reader(messages, count, "gy", members), count, lax.axis_index("gy"))
    ahead, behind = response_ref[1], response_ref[2]
    rows = ahead.shape[0]
    east, north = jnp.zeros_like(ahead), jnp.zeros_like(ahead)
    for k in range(members):
        filtered = local_ref[k] + ahead * entering[:, k : k + 1] + behind * backward[:, k : k + 1]
        east += anomalies_ref[0, k].astype(jnp.float32) * filtered
        north += anomalies_ref[1, k].astype(jnp.float32) * filtered
    out_ref[:rows] = east * spread
    out_ref[rows:] = north * spread


def fourth_kernel(members, spread, shares, *refs):
    partials = refs[:shares]
    (
        anomalies_ref,
        columns_ref,
        weights_ref,
        rates_ref,
        response_ref,
        increment_ref,
        out_ref,
        message_ref,
    ) = refs[shares:]
    rates = rates_ref[...]
    rows = rates.shape[0]
    increment = partials[0][...]
    for ref in partials[1:]:
        increment = increment + ref[...]
    increment_ref[...] = increment
    picked = split_dot(increment, columns_ref[...], ((1,), (0,)))
    weights = weights_ref[: 2 * rows]
    values, precisions = weights_ref[2 * rows : 2 * rows + 1], weights_ref[2 * rows + 1 : 2 * rows + 2]
    projected = jnp.sum(weights * picked, axis=0, keepdims=True)
    misfit = precisions * (projected - values)
    back = split_dot(weights * misfit, columns_ref[...], ((1,), (1,)))
    east = back[:rows] * rates * spread
    north = back[rows:] * rates * spread

    def get(k):
        weights = anomalies_ref[0, k].astype(jnp.float32) * east + anomalies_ref[1, k].astype(jnp.float32) * north
        out_ref[k] = weights
        return weights

    send_y(get, members, response_ref, message_ref)


def fifth_kernel(members, count, *refs):
    messages = refs[:-10]
    (
        local_ref,
        response_ref,
        y_rates_ref,
        x_rates_ref,
        x_response_ref,
        controls_ref,
        old_ref,
        old_sum_ref,
        out_ref,
        message_ref,
    ) = refs[-10:]
    entering, backward, _ = chain(y_reader(messages, count, "gy", members), count, lax.axis_index("gy"))
    y_rates, rates = y_rates_ref[...], x_rates_ref[...]
    rows, columns = rates.shape
    factor = rates * jnp.sqrt(1.0 - y_rates * y_rates) / y_rates
    ahead, behind = factor * response_ref[1], factor * response_ref[2]

    def get(k):
        return factor * local_ref[k] + ahead * entering[:, k : k + 1] + behind * backward[:, k : k + 1]

    scales = jnp.sqrt(1.0 - rates * rates)
    ratio = scales / rates
    x_ahead, x_behind = ratio * x_response_ref[members], ratio * x_response_ref[members + 1]
    sums = [jnp.zeros((rows, columns), jnp.float32)]

    def take(k, ahead, back):
        gradient = controls_ref[k] + ratio * back
        out_ref[k] = gradient
        change = gradient - old_ref[k]
        sums[0] += gradient * change
        slope = gradient + change
        message_ref[k : k + 1] = ahead[rows - 1 :]
        message_ref[members + k : members + k + 1] = back[:1]
        message_ref[2 * members + k : 2 * members + k + 1] = jnp.sum(x_ahead * slope, axis=0, keepdims=True)
        message_ref[3 * members + k : 3 * members + k + 1] = jnp.sum(x_behind * slope, axis=0, keepdims=True)

    x_sweeps(get, members, rates, scales, take)
    end = 4 * members
    message_ref[end : end + 1] = jnp.sum(sums[0], axis=0, keepdims=True)
    message_ref[end + 1 : end + 2] = jnp.sum(old_sum_ref[...], axis=0, keepdims=True)
    message_ref[end + 2 :] = jnp.zeros((message_ref.shape[0] - end - 2, columns), jnp.float32)


def sixth_kernel(members, count, *refs):
    local_ref, rates_ref, x_response_ref, gradient_ref, sums_ref, states_ref = refs[-6:]
    messages = refs[: (len(refs) - 6) // 2]
    earlier = refs[len(messages) : -6]
    read, read_earlier = source_reader(messages, count, "gx"), source_reader(earlier, count, "gx")
    half = row_count(members)
    blocks = [read(d) for d in range(count)]
    answers = [read_earlier(d) for d in range(count)]

    def get(d):
        return (
            blocks[d][:members],
            blocks[d][members : 2 * members],
            answers[d][members : members + 1],
            answers[d][half + members : half + members + 1],
        )

    entering, backward, every = chain(get, count, lax.axis_index("gx"), True)
    states_ref[:members] = entering
    states_ref[half : half + members] = backward
    rates = rates_ref[...]
    rows, columns = rates.shape
    factor = jnp.sqrt(1.0 - rates * rates) / rates
    ahead, behind = factor * x_response_ref[members], factor * x_response_ref[members + 1]
    for k in range(members):
        gradient_ref[k] = (
            local_ref[k] + ahead * states_ref[k : k + 1] + behind * states_ref[half + k : half + k + 1]
        )
    total = jnp.zeros((members, columns), jnp.float32)
    numerator, denominator = jnp.zeros((1, columns), jnp.float32), jnp.zeros((1, columns), jnp.float32)
    for d in range(count):
        block, answer = blocks[d], answers[d]
        one, two = every[d]
        squares = [answer[members + n : members + n + 1] for n in (1, 2, 3)]
        total += one * (block[2 * members : 3 * members] + squares[0] * one + squares[1] * two)
        total += two * (block[3 * members : 4 * members] + squares[2] * two)
        numerator += block[4 * members : 4 * members + 1]
        denominator += block[4 * members + 1 : 4 * members + 2]
    numerator += jnp.sum(total, axis=0, keepdims=True)
    row = lax.broadcasted_iota(jnp.int32, (SUB, columns), 0)
    sums = jnp.where(row == 0, numerator, jnp.where(row == 1, denominator, 0.0))
    packed = sums[:, :LANES]
    for at in range(LANES, columns, LANES):
        packed = packed + sums[:, at : at + LANES]
    sums_ref[...] = packed


def last_kernel(*refs):
    near_ref, old_ref, gradient_ref, far_ref, direction_ref, semaphores = refs[-6:]
    copies = [pltpu.make_async_copy(near_ref, gradient_ref, semaphores.at[0])]
    copies[0].start()
    total = refs[0][...]
    for ref in refs[1:-6]:
        total = total + ref[...]
    numerator = jnp.sum(total[:1], axis=1, keepdims=True)
    denominator = jnp.sum(total[1:2], axis=1, keepdims=True)
    ratio = numerator / denominator
    for k in range(near_ref.shape[0]):
        direction_ref[k] = ratio * old_ref[k] - near_ref[k]
    copies.append(pltpu.make_async_copy(direction_ref, far_ref, semaphores.at[1]))
    copies[1].start()
    for copy in copies:
        copy.wait()


def exchange(message, axis, count):
    if count <= 4:
        shifts = range(1, count)
        return [message] + [lax.ppermute(message, axis, [(i, (i + d) % count) for i in range(count)]) for d in shifts]
    return [lax.all_gather(message, axis)]


def shares_over(values, axis, count):
    if count == 2:
        return [values, lax.ppermute(values, axis, [(0, 1), (1, 0)])]
    return [lax.psum(values, axis)]


def shards(
    n_gx,
    n_gy,
    n_gz,
    controls,
    anomalies,
    x_rates,
    y_rates,
    obs_cells,
    obs_codes,
    obs_values,
    obs_weights,
    prev_gradient,
    prev_direction,
):
    members, rows, columns = controls.shape
    spread = 1.0 / math.sqrt(members * n_gz - 1)
    lines = 2 * row_count(members)
    observed = obs_cells.size
    depth = (columns - 1).bit_length()
    field = (members, rows, columns)
    extended = (members + 2, rows, columns)

    near = pltpu.with_memory_space_constraint
    x_response, message = call(
        functools.partial(first_kernel, members),
        (f32(*extended), f32(lines, columns)),
        [pltpu.VMEM(field, jnp.float32), pltpu.VMEM((rows, columns), jnp.float32), pltpu.SemaphoreType.DMA((2,))],
        in_specs=[HBM_SPEC, HBM_SPEC],
    )(near(controls, pltpu.HBM), near(x_rates, pltpu.HBM))
    x_messages = exchange(message, "gx", n_gx)
    forward, reverse, response, column_ones, row_weights, old_sum = call(
        tables_kernel,
        (
            f32(depth, rows, columns),
            f32(depth, rows, columns),
            f32(5, rows, columns),
            jax.ShapeDtypeStruct((columns, observed), jnp.bfloat16),
            f32(2 * rows + SUB, observed),
            f32(rows, columns),
        ),
    )(
        y_rates,
        obs_cells.reshape(1, observed),
        obs_codes.reshape(1, observed),
        obs_values.reshape(1, observed),
        obs_weights.reshape(1, observed),
        prev_gradient,
    )
    weights, message = call(
        functools.partial(second_kernel, members, n_gx),
        (f32(*field), f32(rows, LANES)),
        [pltpu.VMEM((lines, columns), jnp.float32)],
    )(*x_messages, x_response, y_rates, response)
    messages = exchange(message, "gy", n_gy)
    filtered = call(sweep_kernel, f32(*field))(weights, y_rates, forward, reverse)
    partial = call(functools.partial(third_kernel, members, n_gy, spread), f32(2 * rows, columns))(
        *messages, filtered, response, anomalies
    )
    partials = shares_over(partial, "gz", n_gz)
    increment, weights, message = call(
        functools.partial(fourth_kernel, members, spread, len(partials)),
        (f32(2 * rows, columns), f32(*field), f32(rows, LANES)),
    )(*partials, anomalies, column_ones, row_weights, y_rates, response)
    messages = exchange(message, "gy", n_gy)
    pulled = call(sweep_kernel, f32(*field))(weights, y_rates, forward, reverse)
    gradient, message = call(
        functools.partial(fifth_kernel, members, n_gy),
        (f32(*field), f32(-(-(4 * members + 2) // SUB) * SUB, columns)),
    )(*messages, pulled, response, y_rates, x_rates, x_response, controls, prev_gradient, old_sum)
    gradient, sums = call(
        functools.partial(sixth_kernel, members, n_gx),
        (f32(*field), f32(SUB, LANES)),
        [pltpu.VMEM((lines, columns), jnp.float32)],
    )(*exchange(message, "gx", n_gx), *x_messages, gradient, x_rates, x_response)
    sums = sum(shares_over(sums, "gz", n_gz))
    gradient, direction = call(
        last_kernel,
        (f32(*field), f32(*field)),
        [pltpu.VMEM(field, jnp.float32), pltpu.SemaphoreType.DMA((2,))],
        out_specs=(HBM_SPEC, HBM_SPEC),
    )(*shares_over(sums, "gy", n_gy), gradient, prev_direction)
    return gradient, direction, increment.reshape(2, rows, columns)


def solution(mesh):
    in_specs = (
        P("gz", ("grp", "gx"), "gy"),
        P(None, "gz", ("grp", "gx"), "gy"),
        P(("grp", "gx"), "gy"),
        P(("grp", "gx"), "gy"),
        P(("grp", "gx"), "gy", None),
        P(("grp", "gx"), "gy", None),
        P(("grp", "gx"), "gy", None),
        P(("grp", "gx"), "gy", None),
        P("gz", ("grp", "gx"), "gy"),
        P("gz", ("grp", "gx"), "gy"),
    )
    out_specs = (
        P("gz", ("grp", "gx"), "gy"),
        P("gz", ("grp", "gx"), "gy"),
        P(None, ("grp", "gx"), "gy"),
    )
    body = functools.partial(shards, mesh.shape["gx"], mesh.shape["gy"], mesh.shape["gz"])
    return jax.shard_map(body, mesh=mesh, in_specs=in_specs, out_specs=out_specs, check_vma=False)
```

```python
import functools
import math

import jax
import jax.numpy as jnp
from jax import lax
from jax.experimental import pallas as pl
from jax.experimental.pallas import tpu as pltpu
from jax.sharding import PartitionSpec as P

NDIR = 72
SUB = 8
LANES = 128
LIMIT = 8 * 2**20
PIECES = 4
VMEM_SPEC = pl.BlockSpec(memory_space=pltpu.VMEM)
HBM_SPEC = pl.BlockSpec(memory_space=pltpu.HBM)


def call(body, out_shape, scratch=(), flops=100000, moved=100000, **specs):
    return pl.pallas_call(
        body,
        out_shape=out_shape,
        **specs,
        compiler_params=pltpu.CompilerParams(vmem_limit_bytes=LIMIT),
        scratch_shapes=list(scratch),
        cost_estimate=pl.CostEstimate(flops=flops, bytes_accessed=moved, transcendentals=0),
    )


def f32(*shape):
    return jax.ShapeDtypeStruct(shape, jnp.float32)


def first_rows(members):
    return -(-(2 * members + 2) // 4) * 4


def put(ref, row, height, value):
    for n in range(value.shape[1] // LANES):
        ref[n * height + row : n * height + row + 1] = value[:, n * LANES : (n + 1) * LANES]


def block_of(message, start, count, height, columns):
    return jnp.concatenate(
        [message[n * height + start : n * height + start + count] for n in range(columns // LANES)], axis=1
    )


def folded(row):
    total = row[:, :LANES]
    for at in range(LANES, row.shape[1], LANES):
        total = total + row[:, at : at + LANES]
    return total


def chain(get, count, place, everywhere=False):
    first = get(0)
    zero = jnp.zeros_like(first[0])
    if count == 1:
        return zero, zero, [(zero, zero)]
    low, high, low_back, high_back = {}, {}, {}, {}
    state = zero
    for d in range(count - 1, 0, -1):
        low[d] = state
        out, _, product, _ = get(d)
        state = jnp.where(place >= d, out + product * state, state)
    entering = state
    state = first[0] + first[2] * entering
    for d in range(1, count):
        high[d] = state
        if d < count - 1:
            out, _, product, _ = get(count - d)
            state = out + product * state
    state = zero
    for d in range(count - 1, 0, -1):
        high_back[d] = state
        _, out, product, response = get(count - d)
        state = jnp.where(place + d < count, out + response * high[d] + product * state, state)
    backward = state
    if not everywhere:
        return entering, backward, []
    state = first[1] + first[3] * entering + first[2] * backward
    for d in range(1, count):
        low_back[d] = state
        if d < count - 1:
            _, out, product, response = get(d)
            state = out + response * low[d] + product * state
    every = [(entering, backward)]
    for d in range(1, count):
        above = count - d
        every.append(
            (
                jnp.where(place >= d, low[d], high[above]),
                jnp.where(place >= d, low_back[d], high_back[above]),
            )
        )
    return entering, backward, every


def source_reader(refs, count, axis):
    if len(refs) == count:
        return lambda d: refs[d][...]
    place = lax.axis_index(axis)
    return lambda d: refs[0][lax.rem(place - d + count, count)]


def x_reader(refs, count, axis, members, columns):
    read = source_reader(refs, count, axis)
    height = first_rows(members)

    @functools.cache
    def get(d):
        message = read(d)
        return [
            block_of(message, start, rows, height, columns)
            for start, rows in ((0, members), (members, members), (2 * members, 1), (2 * members + 1, 1))
        ]

    return get


def y_reader(refs, count, axis, members):
    read = source_reader(refs, count, axis)
    half = LANES // 2

    @functools.cache
    def get(d):
        block = read(d)
        back = pltpu.roll(block, half, 1)
        return (
            block,
            back,
            jnp.broadcast_to(block[:, members : members + 1], block.shape),
            jnp.broadcast_to(back[:, members : members + 1], block.shape),
        )

    return get


def tables_of(rates, axis, reverse):
    width = rates.shape[axis]
    at = lax.broadcasted_iota(jnp.int32, rates.shape, axis)
    table = jnp.where(at == (width - 1 if reverse else 0), 0.0, rates)
    tables, step = [], 1
    while step < width:
        tables.append(table)
        table = table * pltpu.roll(table, width - step if reverse else step, axis)
        step *= 2
    return tables


def sweep(values, tables, axis, reverse):
    width = values.shape[axis]
    step = 1
    for table in tables:
        values = values + table * pltpu.roll(values, width - step if reverse else step, axis)
        step *= 2
    return values


def responses(rates, scales, axis, forward, reverse):
    at = lax.broadcasted_iota(jnp.int32, rates.shape, axis)
    product = sweep(jnp.where(at == 0, rates, 0.0), forward, axis, False)
    answer = sweep(scales * product, reverse, axis, True)
    behind = sweep(jnp.where(at == rates.shape[axis] - 1, rates, 0.0), reverse, axis, True)
    return product, answer, behind


def x_sweeps(get, count, rates, scales, take):
    forward, reverse = tables_of(rates, 0, False), tables_of(rates, 0, True)
    for k in range(count):
        ahead = sweep(get(k), forward, 0, False)
        take(k, ahead, sweep(scales * ahead, reverse, 0, True))


def send_y(get, count, response_ref, message_ref):
    last, first = response_ref[3], response_ref[4]
    rows, columns = last.shape
    lane = lax.broadcasted_iota(jnp.int32, (rows, LANES), 1)
    half = LANES // 2
    product, answer = response_ref[0][:, columns - 1 :], response_ref[1][:, :1]
    message = jnp.where(lane == count, product, jnp.where(lane == half + count, answer, 0.0))
    for k in range(count):
        weights = get(k)
        message = jnp.where(lane == k, jnp.sum(last * weights, axis=1, keepdims=True), message)
        message = jnp.where(lane == half + k, jnp.sum(first * weights, axis=1, keepdims=True), message)
    message_ref[...] = message


def split_dot(a, b, dims):
    rows = a.shape[0]
    high = a.astype(jnp.bfloat16)
    rest = a - high.astype(jnp.float32)
    middle = rest.astype(jnp.bfloat16)
    low = (rest - middle.astype(jnp.float32)).astype(jnp.bfloat16)
    parts = jnp.concatenate([high, middle, low], axis=0)
    out = lax.dot_general(parts, b, (dims, ((), ())), preferred_element_type=jnp.float32)
    return out[:rows] + (out[rows : 2 * rows] + out[2 * rows :])


def pieces(members):
    size = -(-members // PIECES)
    return [slice(at, min(at + size, members)) for at in range(0, members, size)]


def first_kernel(members, far_controls_ref, far_rates_ref, local_ref, message_ref, controls_ref, rates_ref, semaphores):
    fetches = [pltpu.make_async_copy(far_rates_ref, rates_ref, semaphores.at[0])]
    for n, piece in enumerate(pieces(members)):
        fetches.append(
            pltpu.make_async_copy(far_controls_ref.at[piece], controls_ref.at[piece], semaphores.at[n + 1])
        )
    for fetch in fetches:
        fetch.start()
    fetches[0].wait()
    rates = rates_ref[...]
    rows, columns = rates.shape
    scales = jnp.sqrt(1.0 - rates * rates)
    height = first_rows(members)
    forward, reverse = tables_of(rates, 0, False), tables_of(rates, 0, True)
    product, answer, behind = responses(rates, scales, 0, forward, reverse)
    local_ref[members] = answer
    local_ref[members + 1] = behind
    put(message_ref, 2 * members, height, product[rows - 1 :])
    put(message_ref, 2 * members + 1, height, answer[:1])
    for row in range(2 * members + 2, height):
        put(message_ref, row, height, jnp.zeros((1, columns), jnp.float32))

    def take(k, ahead, back):
        local_ref[k] = back
        put(message_ref, k, height, ahead[rows - 1 :])
        put(message_ref, members + k, height, back[:1])

    for fetch in fetches[1:]:
        fetch.wait()
    x_sweeps(lambda k: scales * controls_ref[k], members, rates, scales, take)


def tables_kernel(
    rates_ref,
    cells_ref,
    codes_ref,
    values_ref,
    precisions_ref,
    old_ref,
    forward_ref,
    reverse_ref,
    response_ref,
    columns_ref,
    places_ref,
    weights_ref,
    old_sum_ref,
):
    rates = rates_ref[...]
    rows, columns = rates.shape
    scales = jnp.sqrt(1.0 - rates * rates)
    forward, reverse = tables_of(rates, 1, False), tables_of(rates, 1, True)
    for n in range(len(forward)):
        forward_ref[n] = forward[n]
        reverse_ref[n] = reverse[n]
    product, answer, behind = responses(rates, scales, 1, forward, reverse)
    lane = lax.broadcasted_iota(jnp.int32, rates.shape, 1)
    response_ref[0] = product
    response_ref[1] = answer
    response_ref[2] = behind
    response_ref[3] = jnp.where(lane == columns - 1, 1.0, pltpu.roll(behind, columns - 1, 1))
    reach = scales * jnp.where(lane == 0, 1.0, pltpu.roll(product, 1, 1))
    carried = sweep(rates * reach, reverse, 1, True)
    response_ref[4] = reach + jnp.where(lane == columns - 1, 0.0, pltpu.roll(carried, columns - 1, 1))
    cells = cells_ref[...]
    count = cells.shape[1]
    at = lax.broadcasted_iota(jnp.int32, (columns, count), 0)
    columns_ref[...] = jnp.where(at == cells % columns, 1.0, 0.0).astype(jnp.bfloat16)
    places_ref[...] = jnp.broadcast_to(cells % columns, (rows, count))
    bearing = codes_ref[...].astype(jnp.float32) * (2.0 * math.pi / NDIR)
    row = lax.broadcasted_iota(jnp.int32, (rows, count), 0) == cells // columns
    weights_ref[:rows] = jnp.where(row, jnp.cos(bearing), 0.0)
    weights_ref[rows : 2 * rows] = jnp.where(row, jnp.sin(bearing), 0.0)
    weights_ref[2 * rows : 2 * rows + 1] = values_ref[...]
    weights_ref[2 * rows + 1 : 2 * rows + 2] = precisions_ref[...]
    total = jnp.zeros((rows, columns), jnp.float32)
    for k in range(old_ref.shape[0]):
        total += old_ref[k] * old_ref[k]
    old_sum_ref[...] = total


def second_kernel(members, count, *refs):
    messages = refs[:-6]
    local_ref, rates_ref, response_ref, out_ref, message_ref, states_ref = refs[-6:]
    place = lax.axis_index("gx")
    columns = rates_ref.shape[1]
    entering, backward, _ = chain(x_reader(messages, count, "gx", members, columns), count, place)
    states_ref[0] = entering
    states_ref[1] = backward
    rates = rates_ref[...]
    scales = jnp.sqrt(1.0 - rates * rates)
    local, ahead, behind = scales, scales * local_ref[members], scales * local_ref[members + 1]

    def get(k):
        weights = (
            local * local_ref[k] + ahead * states_ref[0, k : k + 1] + behind * states_ref[1, k : k + 1]
        )
        out_ref[k] = weights
        return weights

    send_y(get, members, response_ref, message_ref)


def sweep_kernel(weights_ref, rates_ref, forward_ref, reverse_ref, out_ref):
    rates = rates_ref[...]
    scales = jnp.sqrt(1.0 - rates * rates)
    forward = [forward_ref[n] for n in range(forward_ref.shape[0])]
    reverse = [reverse_ref[n] for n in range(reverse_ref.shape[0])]
    for k in range(weights_ref.shape[0]):
        out_ref[k] = sweep(scales * sweep(weights_ref[k], forward, 1, False), reverse, 1, True)


def third_kernel(members, count, spread, *refs):
    messages = refs[:-4]
    local_ref, response_ref, anomalies_ref, out_ref = refs[-4:]
    entering, backward, _ = chain(y_reader(messages, count, "gy", members), count, lax.axis_index("gy"))
    ahead, behind = response_ref[1], response_ref[2]
    rows = ahead.shape[0]
    east, north = jnp.zeros_like(ahead), jnp.zeros_like(ahead)
    for k in range(members):
        filtered = local_ref[k] + ahead * entering[:, k : k + 1] + behind * backward[:, k : k + 1]
        east += anomalies_ref[0, k].astype(jnp.float32) * filtered
        north += anomalies_ref[1, k].astype(jnp.float32) * filtered
    out_ref[:rows] = east * spread
    out_ref[rows:] = north * spread


def fourth_kernel(members, spread, shares, *refs):
    partials = refs[:shares]
    (
        anomalies_ref,
        columns_ref,
        places_ref,
        weights_ref,
        rates_ref,
        response_ref,
        increment_ref,
        out_ref,
        message_ref,
    ) = refs[shares:]
    rates = rates_ref[...]
    rows, columns = rates.shape
    increment = partials[0][...]
    for ref in partials[1:]:
        increment = increment + ref[...]
    increment_ref[...] = increment
    places = places_ref[...]
    lanes, tile = places % LANES, places // LANES
    picked = []
    for start in (0, rows):
        value = jnp.zeros(places.shape, jnp.float32)
        for n in range(columns // LANES):
            block = increment[start : start + rows, n * LANES : (n + 1) * LANES]
            found = [
                jnp.take_along_axis(block, lanes[:, at : at + LANES], axis=1) for at in range(0, places.shape[1], LANES)
            ]
            value = jnp.where(tile == n, jnp.concatenate(found, axis=1), value)
        picked.append(value)
    picked = jnp.concatenate(picked, axis=0)
    weights = weights_ref[: 2 * rows]
    values, precisions = weights_ref[2 * rows : 2 * rows + 1], weights_ref[2 * rows + 1 : 2 * rows + 2]
    projected = jnp.sum(weights * picked, axis=0, keepdims=True)
    misfit = precisions * (projected - values)
    back = split_dot(weights * misfit, columns_ref[...], ((1,), (1,)))
    east = back[:rows] * rates * spread
    north = back[rows:] * rates * spread

    def get(k):
        weights = anomalies_ref[0, k].astype(jnp.float32) * east + anomalies_ref[1, k].astype(jnp.float32) * north
        out_ref[k] = weights
        return weights

    send_y(get, members, response_ref, message_ref)


def fifth_kernel(members, count, *refs):
    messages = refs[:-10]
    (
        local_ref,
        response_ref,
        y_rates_ref,
        x_rates_ref,
        x_response_ref,
        controls_ref,
        old_ref,
        old_sum_ref,
        out_ref,
        message_ref,
    ) = refs[-10:]
    entering, backward, _ = chain(y_reader(messages, count, "gy", members), count, lax.axis_index("gy"))
    y_rates, rates = y_rates_ref[...], x_rates_ref[...]
    rows, columns = rates.shape
    factor = rates * jnp.sqrt(1.0 - y_rates * y_rates) / y_rates
    ahead, behind = factor * response_ref[1], factor * response_ref[2]

    def get(k):
        return factor * local_ref[k] + ahead * entering[:, k : k + 1] + behind * backward[:, k : k + 1]

    scales = jnp.sqrt(1.0 - rates * rates)
    ratio = scales / rates
    x_ahead, x_behind = ratio * x_response_ref[members], ratio * x_response_ref[members + 1]
    sums = [jnp.zeros((rows, columns), jnp.float32)]

    def take(k, ahead, back):
        gradient = controls_ref[k] + ratio * back
        out_ref[k] = gradient
        change = gradient - old_ref[k]
        sums[0] += gradient * change
        slope = gradient + change
        put(message_ref, k, height, ahead[rows - 1 :])
        put(message_ref, members + k, height, back[:1])
        put(message_ref, 2 * members + k, height, jnp.sum(x_ahead * slope, axis=0, keepdims=True))
        put(message_ref, 3 * members + k, height, jnp.sum(x_behind * slope, axis=0, keepdims=True))

    height = 4 * members
    x_sweeps(get, members, rates, scales, take)
    blocks = columns // LANES
    end = blocks * height
    message_ref[end : end + 1] = folded(jnp.sum(sums[0], axis=0, keepdims=True))
    message_ref[end + 1 : end + 2] = folded(jnp.sum(old_sum_ref[...], axis=0, keepdims=True))
    squares = (x_ahead * x_ahead, 2.0 * x_ahead * x_behind, x_behind * x_behind)
    for n, square in enumerate(squares):
        put(message_ref, end + 2 + n * blocks, 1, jnp.sum(square, axis=0, keepdims=True))
    last = end + 2 + len(squares) * blocks
    if last < message_ref.shape[0]:
        message_ref[last:] = jnp.zeros((message_ref.shape[0] - last, LANES), jnp.float32)


def sixth_kernel(members, count, *refs):
    local_ref, rates_ref, x_response_ref, gradient_ref, sums_ref, states_ref = refs[-6:]
    messages = refs[: (len(refs) - 6) // 2]
    earlier = refs[len(messages) : -6]
    read, read_earlier = source_reader(messages, count, "gx"), source_reader(earlier, count, "gx")
    rows, columns = rates_ref.shape
    height, early_height = 4 * members, first_rows(members)
    messages, earlier = [read(d) for d in range(count)], [read_earlier(d) for d in range(count)]
    outs = [[block_of(message, n * members, members, height, columns) for n in range(4)] for message in messages]
    answers = [[block_of(message, 2 * members + n, 1, early_height, columns) for n in range(2)] for message in earlier]

    def get(d):
        return outs[d][0], outs[d][1], answers[d][0], answers[d][1]

    entering, backward, every = chain(get, count, lax.axis_index("gx"), True)
    states_ref[0] = entering
    states_ref[1] = backward
    rates = rates_ref[...]
    factor = jnp.sqrt(1.0 - rates * rates) / rates
    ahead, behind = factor * x_response_ref[members], factor * x_response_ref[members + 1]
    for k in range(members):
        gradient_ref[k] = (
            local_ref[k] + ahead * states_ref[0, k : k + 1] + behind * states_ref[1, k : k + 1]
        )
    total = jnp.zeros((members, columns), jnp.float32)
    sums = jnp.zeros((2, LANES), jnp.float32)
    blocks = columns // LANES
    end = blocks * height
    for d in range(count):
        message = messages[d]
        one, two = every[d]
        squares = [block_of(message, end + 2 + n * blocks, 1, 1, columns) for n in range(3)]
        total += one * (outs[d][2] + squares[0] * one + squares[1] * two)
        total += two * (outs[d][3] + squares[2] * two)
        sums += message[end : end + 2]
    sums_ref[...] = jnp.zeros(sums_ref.shape, jnp.float32)
    sums_ref[:1] = sums[:1] + folded(jnp.sum(total, axis=0, keepdims=True))
    sums_ref[1:2] = sums[1:]


def last_kernel(*refs):
    near_ref, old_ref, gradient_ref, far_ref, direction_ref, semaphores = refs[-6:]
    members = near_ref.shape[0]
    parts = pieces(members)
    copies = []
    for n, piece in enumerate(parts):
        copies.append(pltpu.make_async_copy(near_ref.at[piece], gradient_ref.at[piece], semaphores.at[n]))
        copies[-1].start()
    total = refs[0][...]
    for ref in refs[1:-6]:
        total = total + ref[...]
    total = jnp.sum(total, axis=1, keepdims=True)
    ratio = total[:1] / total[1:2]
    for n, piece in enumerate(parts):
        for k in range(piece.start, piece.stop):
            direction_ref[k] = ratio * old_ref[k] - near_ref[k]
        copies.append(pltpu.make_async_copy(direction_ref.at[piece], far_ref.at[piece], semaphores.at[PIECES + n]))
        copies[-1].start()
    for copy in copies:
        copy.wait()


def exchange(message, axis, count):
    if count <= 4:
        shifts = range(1, count)
        return [message] + [lax.ppermute(message, axis, [(i, (i + d) % count) for i in range(count)]) for d in shifts]
    return [lax.all_gather(message, axis)]


def shares_over(values, axis, count):
    if count == 2:
        return [values, lax.ppermute(values, axis, [(0, 1), (1, 0)])]
    return [lax.psum(values, axis)]


def crossed_shares(values, n_gy, n_gz):
    if n_gy == 2 and n_gz == 2:
        return [values, lax.ppermute(values, ("gy", "gz"), [(i, 3 - i) for i in range(4)])]
    return shares_over(values, "gy", n_gy)


def shards(
    n_gx,
    n_gy,
    n_gz,
    controls,
    anomalies,
    x_rates,
    y_rates,
    obs_cells,
    obs_codes,
    obs_values,
    obs_weights,
    prev_gradient,
    prev_direction,
):
    members, rows, columns = controls.shape
    spread = 1.0 / math.sqrt(members * n_gz - 1)
    blocks = columns // LANES
    lines = blocks * first_rows(members)
    observed = obs_cells.size
    depth = (columns - 1).bit_length()
    field = (members, rows, columns)
    extended = (members + 2, rows, columns)

    near = pltpu.with_memory_space_constraint
    x_response, message = call(
        functools.partial(first_kernel, members),
        (f32(*extended), f32(lines, LANES)),
        [pltpu.VMEM(field, jnp.float32), pltpu.VMEM((rows, columns), jnp.float32), pltpu.SemaphoreType.DMA((PIECES + 1,))],
        in_specs=[HBM_SPEC, HBM_SPEC],
    )(near(controls, pltpu.HBM), near(x_rates, pltpu.HBM))
    x_messages = exchange(message, "gx", n_gx)
    forward, reverse, response, column_ones, places, row_weights, old_sum = call(
        tables_kernel,
        (
            f32(depth, rows, columns),
            f32(depth, rows, columns),
            f32(5, rows, columns),
            jax.ShapeDtypeStruct((columns, observed), jnp.bfloat16),
            jax.ShapeDtypeStruct((rows, observed), jnp.int32),
            f32(2 * rows + SUB, observed),
            f32(rows, columns),
        ),
    )(
        y_rates,
        obs_cells.reshape(1, observed),
        obs_codes.reshape(1, observed),
        obs_values.reshape(1, observed),
        obs_weights.reshape(1, observed),
        prev_gradient,
    )
    weights, message = call(
        functools.partial(second_kernel, members, n_gx),
        (f32(*field), f32(rows, LANES)),
        [pltpu.VMEM((2, members, columns), jnp.float32)],
    )(*x_messages, x_response, y_rates, response)
    messages = exchange(message, "gy", n_gy)
    filtered = call(sweep_kernel, f32(*field))(weights, y_rates, forward, reverse)
    partial = call(functools.partial(third_kernel, members, n_gy, spread), f32(2 * rows, columns))(
        *messages, filtered, response, anomalies
    )
    partials = shares_over(partial, "gz", n_gz)
    increment, weights, message = call(
        functools.partial(fourth_kernel, members, spread, len(partials)),
        (f32(2 * rows, columns), f32(*field), f32(rows, LANES)),
    )(*partials, anomalies, column_ones, places, row_weights, y_rates, response)
    messages = exchange(message, "gy", n_gy)
    pulled = call(sweep_kernel, f32(*field))(weights, y_rates, forward, reverse)
    gradient, message = call(
        functools.partial(fifth_kernel, members, n_gy),
        (f32(*field), f32(-(-(blocks * (4 * members + 3) + 2) // SUB) * SUB, LANES)),
    )(*messages, pulled, response, y_rates, x_rates, x_response, controls, prev_gradient, old_sum)
    gradient, sums = call(
        functools.partial(sixth_kernel, members, n_gx),
        (f32(*field), f32(SUB, LANES)),
        [pltpu.VMEM((2, members, columns), jnp.float32)],
    )(*exchange(message, "gx", n_gx), *x_messages, gradient, x_rates, x_response)
    sums = sum(shares_over(sums, "gz", n_gz))
    gradient, direction = call(
        last_kernel,
        (f32(*field), f32(*field)),
        [pltpu.VMEM(field, jnp.float32), pltpu.SemaphoreType.DMA((2 * PIECES,))],
        out_specs=(HBM_SPEC, HBM_SPEC),
    )(*crossed_shares(sums, n_gy, n_gz), gradient, prev_direction)
    return gradient, direction, increment.reshape(2, rows, columns)


def solution(mesh):
    in_specs = (
        P("gz", ("grp", "gx"), "gy"),
        P(None, "gz", ("grp", "gx"), "gy"),
        P(("grp", "gx"), "gy"),
        P(("grp", "gx"), "gy"),
        P(("grp", "gx"), "gy", None),
        P(("grp", "gx"), "gy", None),
        P(("grp", "gx"), "gy", None),
        P(("grp", "gx"), "gy", None),
        P("gz", ("grp", "gx"), "gy"),
        P("gz", ("grp", "gx"), "gy"),
    )
    out_specs = (
        P("gz", ("grp", "gx"), "gy"),
        P("gz", ("grp", "gx"), "gy"),
        P(None, ("grp", "gx"), "gy"),
    )
    body = functools.partial(shards, mesh.shape["gx"], mesh.shape["gy"], mesh.shape["gz"])
    return jax.shard_map(body, mesh=mesh, in_specs=in_specs, out_specs=out_specs, check_vma=False)
```
